32 devices in a mesh: dp: 2 (over x), mp: 16 (over z, y, core).
Axes of the slice: x: 2, y: 2, z: 4, core: 2. Of those that a mesh axis runs over, the one named last changes fastest.
Arguments:
- tokens: bfloat16 [32, 512, 768], P(('dp', 'mp')), may hold values from -6 to 6
- segment_ids: int32 [32, 512], P(('dp', 'mp')), may hold values from 0 to 3, never falling along the last dimension, each value on 1 to 256 neighbouring positions
- swap_step: int32 [1], replicated, may hold values from 0 to 1023
- feature_bank: bfloat16 [8, 12, 64, 64], replicated, may hold values from -5 to 5
- query_weight: bfloat16 [768, 768], replicated, may hold values from -0.21875 to 0.21875
- query_bias: bfloat16 [768], replicated, may hold values from -1.5 to 1.5
- key_weight: bfloat16 [768, 768], replicated, may hold values from -0.21875 to 0.21875
- value_weight: bfloat16 [768, 768], replicated, may hold values from -0.21875 to 0.21875
- value_bias: bfloat16 [768], replicated, may hold values from -1.5 to 1.5
- out_weight: bfloat16 [768, 768], replicated, may hold values from -0.875 to 0.875
- out_bias: bfloat16 [768], replicated, may hold values from -1.5 to 1.5
- position_logits: bfloat16 [12, 1023], replicated, may hold values from -3 to 3
- first_gain: bfloat16 [768], replicated, may hold values from 0.5 to 1.5
- first_shift: bfloat16 [768], replicated, may hold values from -1.5 to 1.5
- up_weight: bfloat16 [768, 3072], P(None, 'mp'), may hold values from -0.21875 to 0.21875
- up_bias: bfloat16 [3072], P('mp'), may hold values from -1.5 to 1.5
- down_weight: bfloat16 [3072, 768], P('mp'), may hold values from -0.109375 to 0.109375
- down_bias: bfloat16 [768], replicated, may hold values from -1.5 to 1.5
- second_gain: bfloat16 [768], replicated, may hold values from 0.5 to 1.5
- second_shift: bfloat16 [768], replicated, may hold values from -1.5 to 1.5
- out_cotangent: bfloat16 [32, 512, 768], P(('dp', 'mp')), may hold values from -6 to 6
Outputs:
- layer_out: bfloat16 [32, 512, 768], P(('dp', 'mp'))
- grad_tokens: float32 [32, 512, 768], P(('dp', 'mp'))
- grad_query_weight: float32 [768, 768], replicated
- grad_query_bias: float32 [768], replicated
- grad_key_weight: float32 [768, 768], replicated
- grad_value_weight: float32 [768, 768], replicated
- grad_value_bias: float32 [768], replicated
- grad_out_weight: float32 [768, 768], replicated
- grad_out_bias: float32 [768], replicated
- grad_position_logits: float32 [12, 1023], replicated
- grad_first_gain: float32 [768], replicated
- grad_first_shift: float32 [768], replicated
- grad_up_weight: float32 [768, 3072], P(None, 'mp')
- grad_up_bias: float32 [3072], P('mp')
- grad_down_weight: float32 [3072, 768], P('mp')
- grad_down_bias: float32 [768], replicated
- grad_second_gain: float32 [768], replicated
- grad_second_shift: float32 [768], replicated
The draws below stay inside these ranges and needn't reach their ends.
Inputs may be any that keep to these rules, and one draw needn't show every extreme that they name: `segment_ids`: within each row the ids never fall; a document holds at most 256 tokens.
All inputs are finite; a program needn't handle non-finite values.
Results may differ from the reference program's by a relative error of at most 0.02.
Values may be sent and summed in bfloat16 or wider, within the bound.
No kernel may reach another device: no remote copies, remote signals or barrier semaphores. Data moves between devices by JAX's collectives and lax.ppermute only.
A program may use at most 320 MiB of HBM per device.

```python
import math
import jax
import jax.numpy as jnp
import numpy as np
from jax import lax

D = 768
HEADS = 12
HEAD = 64
FF = 3072
FEAT = 64
SEQ = 512
DOCS = 4
BANKS = 8
ROWS = 32


def levels(stream_key, shape, split, low, largest):
    def one(position, blocks):
        heights = jax.random.uniform(jax.random.fold_in(jax.random.fold_in(stream_key, 6), position), (blocks,), jnp.float32, low / len(split), largest / len(split))
        return jnp.repeat(jnp.exp(heights), shape[position] // blocks).reshape((-1,) + (1,) * (len(shape) - position - 1))

    factor_of = one(*split[0])
    for cut in split[1:]:
        factor_of = factor_of * one(*cut)
    return factor_of


def profile(number_of, total, limit, slope):
    weights = [(1 << 20) // math.isqrt(standing ** slope) + 1 for standing in range(2, number_of + 1)]
    rest, counts = total - limit - (number_of - 1), [1] * (number_of - 1)
    while rest > 0:
        candidates = [i for i in range(number_of - 1) if counts[i] < limit]
        pool, left = sum([weights[i] for i in candidates]), rest
        for i in candidates:
            more = min(limit - counts[i], max(1, left * weights[i] // pool), rest)
            counts[i] = counts[i] + more
            rest = rest - more
    return np.array([limit] + counts)


def ragged_sizes(stream_key, amount, total, reach, lean):
    if amount == 2:
        one = jax.random.randint(stream_key, (), max(1, total - reach), min(reach, total - 1) + 1)
        return jnp.stack([one, total - one])
    tallies = jnp.asarray(profile(amount, total, reach, lean), jnp.int32)
    pairs = (amount - 1) // 2
    donor, taker = tallies[1:1 + 2 * pairs:2], tallies[2:2 + 2 * pairs:2]
    room = jnp.minimum(donor - 1, reach - taker)
    shifted = jax.random.randint(jax.random.fold_in(stream_key, 1), (pairs,), 0, 1 << 20) % (room + 1)
    tallies = tallies.at[1:1 + 2 * pairs:2].set(donor - shifted).at[2:2 + 2 * pairs:2].set(taker + shifted)
    return tallies[jax.random.permutation(jax.random.fold_in(stream_key, 2), amount)]


def bell_draw(stream_key, dims, scale, most, shards=(), kind=jnp.bfloat16):
    gain = levels(stream_key, dims, shards, -0.22, 0.18) if shards else 1.0
    result = jax.random.normal(stream_key, dims, jnp.float32) * scale * gain
    return jnp.minimum(jnp.maximum(result, -most), most).astype(kind)


def setup_inputs(seed: int = 0) -> dict:
    arg_keys = jax.random.split(jax.random.key(seed), 22)
    return {
        "tokens": bell_draw(arg_keys[0], (ROWS, SEQ, D), 1.0, 6.0, ((0, 32),)),
        "segment_ids": jax.vmap(lambda own: jnp.searchsorted(jnp.cumsum(ragged_sizes(own, DOCS, SEQ, SEQ // 2, 0)), jnp.arange(SEQ), side="right"))(jax.random.split(arg_keys[1], ROWS)).reshape((ROWS, SEQ)).astype(jnp.int32),
        "swap_step": jax.random.randint(arg_keys[2], (1,), 0, 1024).astype(jnp.int32),
        "feature_bank": bell_draw(arg_keys[3], (BANKS, HEADS, HEAD, FEAT), 1.0, 5.0),
        "query_weight": bell_draw(arg_keys[4], (D, D), D ** -0.5, 0.21875),
        "query_bias": bell_draw(arg_keys[5], (D,), 0.3, 1.5),
        "key_weight": bell_draw(arg_keys[6], (D, D), D ** -0.5, 0.21875),
        "value_weight": bell_draw(arg_keys[7], (D, D), D ** -0.5, 0.21875),
        "value_bias": bell_draw(arg_keys[8], (D,), 0.3, 1.5),
        "out_weight": bell_draw(arg_keys[9], (D, D), (D // 16) ** -0.5, 0.875),
        "out_bias": bell_draw(arg_keys[10], (D,), 0.3, 1.5),
        "position_logits": bell_draw(arg_keys[11], (HEADS, 2 * SEQ - 1), 1.0, 3.0),
        "first_gain": jnp.clip(1.0 + 0.1 * jax.random.normal(arg_keys[12], (D,), jnp.float32), 0.5, 1.5).astype(jnp.bfloat16),
        "first_shift": bell_draw(arg_keys[13], (D,), 0.3, 1.5),
        "up_weight": bell_draw(arg_keys[14], (D, FF), D ** -0.5, 0.21875, ((1, 16),)),
        "up_bias": bell_draw(arg_keys[15], (FF,), 0.3, 1.5, ((0, 16),)),
        "down_weight": bell_draw(arg_keys[16], (FF, D), FF ** -0.5, 0.109375, ((0, 16),)),
        "down_bias": bell_draw(arg_keys[17], (D,), 0.3, 1.5),
        "second_gain": jnp.clip(1.0 + 0.1 * jax.random.normal(arg_keys[18], (D,), jnp.float32), 0.5, 1.5).astype(jnp.bfloat16),
        "second_shift": bell_draw(arg_keys[19], (D,), 0.3, 1.5),
        "out_cotangent": bell_draw(arg_keys[20], (ROWS, SEQ, D), 1.0, 6.0, ((0, 32),)),
    }


@jax.custom_vjp
def low(v):
    return lax.optimization_barrier(v.astype(jnp.bfloat16)).astype(jnp.float32)

@jax.custom_vjp
def low_back(v):
    return v

def low_keep(v):
    return (low(v), None)

def low_pass(kept, grad):
    return (grad,)

def back_keep(v):
    return (v, None)

def back_low(kept, grad):
    return (low(grad),)
low.defvjp(low_keep, low_pass)
low_back.defvjp(back_keep, back_low)
EPSILON = 1e-05
PRECISE = lax.Precision.HIGHEST

def matmul(left_side, right_side):
    return jnp.dot(left_side, right_side, precision=PRECISE)

def layer_norm(inputs, factor, offset):
    centre = inputs - lax.optimization_barrier(jnp.mean(inputs, axis=-1, keepdims=True))
    spread = lax.optimization_barrier(jnp.mean(centre * centre, axis=-1, keepdims=True))
    return centre * lax.rsqrt(spread + EPSILON) * factor + offset

def lift(row_block, projection):
    lifted = low_back(jnp.einsum('lhd,hdm->hlm', row_block, projection, precision=PRECISE))
    squares = lax.optimization_barrier(jnp.sum(row_block * row_block, axis=-1)).T
    return low(low_back(jnp.exp(lifted - 0.5 * squares[:, :, None]) * FEAT ** (-0.5)))

def reference(tokens, segment_ids, swap_step, feature_bank, query_weight, query_bias, key_weight, value_weight, value_bias, out_weight, out_bias, position_logits, first_gain, first_shift, up_weight, up_bias, down_weight, down_bias, second_gain, second_shift, out_cotangent):
    projection = lax.dynamic_index_in_dim(feature_bank, swap_step[0] % BANKS, 0, keepdims=False).astype(jnp.float32)
    positions = jnp.arange(SEQ, dtype=jnp.int32)
    offsets = SEQ - 1 + positions[:, None] - positions[None, :]
    query_scale = HEAD ** (-0.25)

    def forward(params):
        token_rows, w_query, b_query, w_key, w_value, b_value, w_out, b_out, logits, gain_one, shift_one, w_up, b_up, w_down, b_down, gain_two, shift_two = params
        flat_rows = token_rows.reshape(ROWS * SEQ, D)
        queries = low(low_back((matmul(flat_rows, w_query) + b_query) * query_scale)).reshape(ROWS, SEQ, HEADS, HEAD)
        keys_all = low(low_back(matmul(flat_rows, w_key) * query_scale)).reshape(ROWS, SEQ, HEADS, HEAD)
        values = low(low_back(matmul(flat_rows, w_value) + b_value)).reshape(ROWS, SEQ, HEADS, HEAD)
        toeplitz_table = jnp.exp(logits)[:, offsets]

        def attend(pieces):
            row_queries, row_keys, row_values, row_segments = pieces
            same_doc = (row_segments[:, None] == row_segments[None, :]).astype(jnp.float32)
            kernel = low_back(jnp.einsum('hlm,hkm->hlk', lift(row_queries, projection), lift(row_keys, projection), precision=PRECISE))
            weights = kernel * toeplitz_table * same_doc[None]
            denominator = lax.optimization_barrier(jnp.sum(weights, axis=-1))
            numerator = low_back(jnp.einsum('hlk,khd->lhd', low(weights), row_values, precision=PRECISE))
            return numerator / denominator.T[:, :, None]
        mixed_out = lax.map(jax.checkpoint(attend), (queries, keys_all, values, segment_ids))
        mixed_out = low(low_back(mixed_out.reshape(ROWS * SEQ, D)))
        branch = low_back(matmul(mixed_out, w_out) + b_out)
        hidden = layer_norm(flat_rows + branch, gain_one, shift_one)
        upward = low_back(matmul(low(hidden), w_up) + b_up)
        activated = low(jax.nn.gelu(upward, approximate=False))
        feed_out = low_back(matmul(activated, w_down))
        return layer_norm(hidden + feed_out + b_down, gain_two, shift_two).reshape(ROWS, SEQ, D)
    floats = tuple((item.astype(jnp.float32) for item in (tokens, query_weight, query_bias, key_weight, value_weight, value_bias, out_weight, out_bias, position_logits, first_gain, first_shift, up_weight, up_bias, down_weight, down_bias, second_gain, second_shift)))
    layer_out, pullback = jax.vjp(forward, floats)
    grads = pullback(out_cotangent.astype(jnp.float32))[0]
    return (layer_out.astype(jnp.bfloat16), grads[0], grads[1], grads[2], grads[3], grads[4], grads[5], grads[6], grads[7], grads[8], grads[9], grads[10], grads[11], grads[12], grads[13], grads[14], grads[15], grads[16])
```

```python
import functools
import jax
import jax.numpy as jnp
from jax import lax
from jax.experimental import pallas as pl
from jax.experimental.pallas import tpu as pltpu
from jax.sharding import PartitionSpec as P

LANES = 128
LOW = jnp.bfloat16


def dot_last(left_side, right_side):
    return lax.dot_general(
        left_side, right_side, (((1,), (1,)), ((), ())), preferred_element_type=jnp.float32
    )


def dot_first(left_side, right_side):
    return lax.dot_general(
        left_side, right_side, (((0,), (0,)), ((), ())), preferred_element_type=jnp.float32
    )


def split_low(wide):
    high = wide.astype(LOW)
    return high, (wide - high.astype(jnp.float32)).astype(LOW)


def key_span(block, blocks, reach):
    first = max(0, block - reach)
    last = min(blocks, block + reach + 1)
    return first * LANES, last * LANES


def features(rows, lift_matrix, gain):
    wide = rows.astype(jnp.float32)
    high, rest = split_low(wide * wide)
    stacked = jnp.concatenate([rows, high, rest], axis=1)
    lifted = jnp.dot(stacked, lift_matrix, preferred_element_type=jnp.float32)
    return jnp.exp(lifted) * gain


def strip(entry_row):
    return pltpu.roll(
        jnp.broadcast_to(entry_row, (LANES, entry_row.shape[1])), 0, 1, stride=1, stride_axis=0
    )


def unstrip(total):
    width = total.shape[1]
    half = total.shape[0] // 2
    while half >= 8:
        total = total[:half] + pltpu.roll(total[half:], width - half, 1)
        half //= 2
    row = lax.broadcasted_iota(jnp.int32, total.shape, 0)
    for step in (4, 2, 1):
        total = jnp.where((row & step) != 0, pltpu.roll(total, width - step, 1), total)
    return jnp.sum(total, axis=0, keepdims=True)


def masked_strip(strip_ref, head, seg_col, seg_row, block, blocks, reach):
    first, last = key_span(block, blocks, reach)
    shift = (blocks - 1 - block) * LANES
    columns = seg_col[block * LANES : (block + 1) * LANES]
    same = jnp.concatenate(
        [
            columns == seg_row[:, start : start + LANES]
            for start in range(first, last, LANES)
        ],
        axis=1,
    )
    return jnp.where(same, strip_ref[head, :, first + shift : last + shift], 0.0)


def attend_kernel(
    head_size, reach, q_ref, k_ref, v_ref, col_ref, row_ref, lift_ref, entry_ref,
    mixed_ref, inverse_ref, strip_ref,
):
    length = q_ref.shape[0]
    blocks = length // LANES
    gain = head_size ** (-0.5)
    for head in range(2):
        strip_ref[head] = strip(entry_ref[0, head : head + 1])
    lift_matrix = lift_ref[0]
    query_low = features(q_ref[...], lift_matrix, gain).astype(LOW)
    key_low = features(k_ref[...], lift_matrix, gain).astype(LOW)
    extended = jnp.concatenate([v_ref[...], jnp.ones((length, LANES), LOW)], axis=1)
    lane = lax.broadcasted_iota(jnp.int32, (LANES, LANES), 1)
    seg_row = row_ref[0]
    seg_col = col_ref[0]
    for block in range(blocks):
        first, last = key_span(block, blocks, reach)
        here = slice(block * LANES, (block + 1) * LANES)
        outs = []
        for head in range(2):
            mine = (lane < head_size) == (head == 0)
            block_query = jnp.where(mine, query_low[here], jnp.zeros((), LOW))
            kernel = dot_last(block_query, key_low[first:last])
            weights = kernel * masked_strip(strip_ref, head, seg_col, seg_row, block, blocks, reach)
            outs.append(
                jnp.dot(
                    weights.astype(LOW), extended[first:last], preferred_element_type=jnp.float32
                )
            )
        both = jnp.where(
            jnp.concatenate([lane, lane], axis=1) % LANES < head_size, outs[0], outs[1]
        )
        inverse = 1.0 / both[:, LANES:]
        mixed_ref[here, :] = (both[:, :LANES] * inverse).astype(LOW)
        inverse_ref[here, :] = inverse


def attend_back_kernel(
    head_size, reach, q_ref, k_ref, v_ref, g_ref, mixed_ref, inverse_ref, col_ref, row_ref,
    lift_ref, back_ref, sums_ref, entry_ref,
    gq_ref, gk_ref, gv_ref, logit_ref, strip_ref, diag_ref, value_acc, key_acc,
):
    length = q_ref.shape[0]
    blocks = length // LANES
    gain = head_size ** (-0.5)
    for head in range(2):
        strip_ref[head] = strip(entry_ref[0, head : head + 1])

    @pl.when(pl.program_id(1) == 0)
    def _():
        diag_ref[...] = jnp.zeros_like(diag_ref)

    lift_matrix = lift_ref[0]
    query_feat = features(q_ref[...], lift_matrix, gain)
    key_feat = features(k_ref[...], lift_matrix, gain)
    query_low = query_feat.astype(LOW)
    key_low = key_feat.astype(LOW)
    values = v_ref[...]
    grad_numer = g_ref[...].astype(jnp.float32) * inverse_ref[...]
    grad_low = grad_numer.astype(LOW)
    high, rest = split_low(grad_numer * mixed_ref[...].astype(jnp.float32))
    grad_denom = jnp.dot(
        jnp.concatenate([high, rest], axis=1), sums_ref[...], preferred_element_type=jnp.float32
    )
    lane = lax.broadcasted_iota(jnp.int32, (LANES, LANES), 1)
    seg_row = row_ref[0]
    seg_col = col_ref[0]
    value_acc[...] = jnp.zeros_like(value_acc)
    key_acc[...] = jnp.zeros_like(key_acc)
    grad_qfeat = []
    for block in range(blocks):
        first, last = key_span(block, blocks, reach)
        shift = (blocks - 1 - block) * LANES
        here = slice(block * LANES, (block + 1) * LANES)
        outs = []
        for head in range(2):
            mine = (lane < head_size) == (head == 0)
            block_query = jnp.where(mine, query_low[here], jnp.zeros((), LOW))
            block_grad = jnp.where(mine, grad_low[here], jnp.zeros((), LOW))
            table = masked_strip(strip_ref, head, seg_col, seg_row, block, blocks, reach)
            weights = dot_last(block_query, key_low[first:last]) * table
            denom = grad_denom[here, head * LANES : (head + 1) * LANES]
            grad_weights = dot_last(block_grad, values[first:last]) - jnp.concatenate(
                [denom] * ((last - first) // LANES), axis=1
            )
            grad_kernel = (grad_weights * table).astype(LOW)
            diag_ref[head, :, first + shift : last + shift] += grad_weights * weights
            value_acc[first:last] += dot_first(weights.astype(LOW), block_grad)
            outs.append(
                jnp.dot(grad_kernel, key_low[first:last], preferred_element_type=jnp.float32)
            )
            key_acc[first:last] += dot_first(grad_kernel, block_query)
        grad_qfeat.append(jnp.where(lane < head_size, outs[0], outs[1]))
    gv_ref[...] = value_acc[...].astype(LOW)

    def lift_back(rows, feature, grad_feature):
        product = grad_feature * feature
        high, rest = split_low(product)
        both = jnp.dot(
            jnp.concatenate([high, rest], axis=1), back_ref[0], preferred_element_type=jnp.float32
        )
        return (both[:, :LANES] - rows.astype(jnp.float32) * both[:, LANES:]).astype(LOW)

    gq_ref[...] = lift_back(q_ref[...], query_feat, jnp.concatenate(grad_qfeat, axis=0))
    gk_ref[...] = lift_back(k_ref[...], key_feat, key_acc[...])
    logit_ref[0] = jnp.concatenate([unstrip(diag_ref[head]) for head in range(2)], axis=0)


def pair_matrices(projection):
    heads, head_size, feat = projection.shape
    pairs = projection.reshape(heads // 2, 2, head_size, feat)
    zero = jnp.zeros_like(pairs[:, 0])
    top = jnp.concatenate([pairs[:, 0], zero], axis=2)
    bottom = jnp.concatenate([zero, pairs[:, 1]], axis=2)
    diagonal = jnp.concatenate([top, bottom], axis=1)
    half = jnp.arange(2 * head_size) // head_size
    ones = jnp.broadcast_to(
        (half[:, None] == half[None, :]).astype(LOW), (heads // 2, 2 * head_size, 2 * feat)
    )
    lift_matrix = jnp.concatenate([diagonal, -0.5 * ones, -0.5 * ones], axis=1).astype(LOW)
    turned = jnp.swapaxes(diagonal, 1, 2)
    back_matrix = jnp.concatenate(
        [
            jnp.concatenate([turned, ones], axis=2),
            jnp.concatenate([jnp.zeros_like(turned), ones], axis=2),
        ],
        axis=1,
    )
    picked = (half[:, None] == (jnp.arange(4 * head_size) // (2 * head_size))[None, :]).astype(LOW)
    sums = jnp.concatenate([picked, picked], axis=0)
    return lift_matrix, back_matrix, sums


def entry_rows(position_logits):
    heads, span = position_logits.shape
    entries = jnp.exp(position_logits.astype(jnp.float32))
    padded = jnp.concatenate([entries, jnp.zeros((heads, 1), jnp.float32)], axis=1)
    turned = jnp.roll(padded[:, ::-1], -LANES, axis=1)
    return turned.reshape(heads // 2, 2, span + 1)


def entry_grads(turned):
    pairs, _, width = turned.shape
    flat = turned.reshape(2 * pairs, width)
    return jnp.roll(flat[:, ::-1], -LANES, axis=1)[:, : width - 1]


def attend(queries, keys, values, seg_col, seg_row, lift_matrix, entries, head_size, reach, rows):
    total, width = queries.shape
    length = total // rows
    pairs = width // LANES
    tile = pl.BlockSpec((length, LANES), lambda p, r: (r, p))
    specs = [
        tile, tile, tile,
        pl.BlockSpec((1, length, LANES), lambda p, r: (r, 0, 0)),
        pl.BlockSpec((1, 1, length), lambda p, r: (r, 0, 0)),
        pl.BlockSpec((1,) + lift_matrix.shape[1:], lambda p, r: (p, 0, 0)),
        pl.BlockSpec((1,) + entries.shape[1:], lambda p, r: (p, 0, 0)),
    ]
    return pl.pallas_call(
        functools.partial(attend_kernel, head_size, reach),
        grid=(pairs, rows),
        in_specs=specs,
        out_specs=[tile, tile],
        out_shape=[
            jax.ShapeDtypeStruct((total, width), LOW),
            jax.ShapeDtypeStruct((total, width), jnp.float32),
        ],
        scratch_shapes=[pltpu.VMEM((2, LANES, entries.shape[2]), jnp.float32)],
        name="attend",
    )(queries, keys, values, seg_col, seg_row, lift_matrix, entries)


def attend_back(
    queries, keys, values, grads, mixed, inverse, seg_col, seg_row, lift_matrix, back_matrix,
    sums, entries, head_size, reach, rows,
):
    total, width = queries.shape
    length = total // rows
    pairs = width // LANES
    tile = pl.BlockSpec((length, LANES), lambda p, r: (r, p))
    specs = [
        tile, tile, tile, tile, tile, tile,
        pl.BlockSpec((1, length, LANES), lambda p, r: (r, 0, 0)),
        pl.BlockSpec((1, 1, length), lambda p, r: (r, 0, 0)),
        pl.BlockSpec((1,) + lift_matrix.shape[1:], lambda p, r: (p, 0, 0)),
        pl.BlockSpec((1,) + back_matrix.shape[1:], lambda p, r: (p, 0, 0)),
        pl.BlockSpec(sums.shape, lambda p, r: (0, 0)),
        pl.BlockSpec((1,) + entries.shape[1:], lambda p, r: (p, 0, 0)),
    ]
    low_out = jax.ShapeDtypeStruct((total, width), LOW)
    span = entries.shape[2]
    return pl.pallas_call(
        functools.partial(attend_back_kernel, head_size, reach),
        grid=(pairs, rows),
        in_specs=specs,
        out_specs=[tile, tile, tile, pl.BlockSpec((1, 2, span), lambda p, r: (p, 0, 0))],
        out_shape=[low_out, low_out, low_out, jax.ShapeDtypeStruct((pairs, 2, span), jnp.float32)],
        scratch_shapes=[
            pltpu.VMEM((2, LANES, span), jnp.float32),
            pltpu.VMEM((2, LANES, span), jnp.float32),
            pltpu.VMEM((length, LANES), jnp.float32),
            pltpu.VMEM((length, LANES), jnp.float32),
        ],
        name="attend_back",
    )(
        queries, keys, values, grads, mixed, inverse, seg_col, seg_row, lift_matrix, back_matrix,
        sums, entries,
    )


EPSILON = 1e-05


def normalize(inputs, factor, offset):
    centre = inputs - jnp.mean(inputs, axis=-1, keepdims=True)
    spread = jnp.mean(centre * centre, axis=-1, keepdims=True)
    inverse = lax.rsqrt(spread + EPSILON)
    normed = centre * inverse
    return (normed * factor + offset, normed, inverse)


def norm_back(upstream, normed, inverse, factor):
    scaled = upstream * factor
    inner = (
        scaled
        - jnp.mean(scaled, axis=-1, keepdims=True)
        - normed * jnp.mean(scaled * normed, axis=-1, keepdims=True)
    )
    return (inverse * inner, jnp.sum(upstream * normed, axis=0), jnp.sum(upstream, axis=0))


SWAP = [(0, 1), (1, 0)]
GROUP = ("dp", "mq")


def other(array):
    return lax.ppermute(array, "core", SWAP)


def share_pieces(array):
    piece = array.shape[0] // lax.axis_size("dp")
    mine = lax.dynamic_slice_in_dim(array, lax.axis_index("dp") * piece, piece, 0)
    return lax.all_gather(mine, GROUP, axis=0, tiled=True)


def scatter_pieces(array):
    mine = lax.psum_scatter(array.astype(LOW), GROUP, scatter_dimension=0, tiled=True)
    return lax.all_gather(mine, "dp", axis=0, tiled=True).astype(jnp.float32)


def sum_everywhere(array):
    half = array.shape[0] // 2
    core = lax.axis_index("core")
    low = array.astype(LOW)
    keep = lax.dynamic_slice_in_dim(low, core * half, half, 0)
    give = lax.dynamic_slice_in_dim(low, (1 - core) * half, half, 0)
    pair = (keep.astype(jnp.float32) + other(give).astype(jnp.float32)).astype(LOW)
    mine = lax.psum_scatter(pair, GROUP, scatter_dimension=0, tiled=True)
    whole = lax.all_gather(mine, GROUP, axis=0, tiled=True)
    theirs = other(whole)
    first = jnp.where(core == 0, whole, theirs)
    second = jnp.where(core == 0, theirs, whole)
    return jnp.concatenate([first, second], axis=0).astype(jnp.float32)


def pack_rows(vectors, width, multiple):
    flat = jnp.concatenate([v.reshape(-1) for v in vectors])
    rows = -(-flat.shape[0] // (width * multiple)) * multiple
    return jnp.pad(flat, (0, rows * width - flat.shape[0])).reshape(rows, width)


def unpack_rows(packed, shapes):
    flat = packed.reshape(-1)
    out, at = [], 0
    for shape in shapes:
        size = 1
        for extent in shape:
            size *= extent
        out.append(flat[at : at + size].reshape(shape))
        at += size
    return out


def local(
    tokens,
    segment_ids,
    swap_step,
    feature_bank,
    query_weight,
    query_bias,
    key_weight,
    value_weight,
    value_bias,
    out_weight,
    out_bias,
    position_logits,
    first_gain,
    first_shift,
    up_weight,
    up_bias,
    down_weight,
    down_bias,
    second_gain,
    second_shift,
    out_cotangent,
):
    rows_here, length, model_width = tokens.shape
    head_count = position_logits.shape[0]
    head_size = model_width // head_count
    query_scale = head_size ** (-0.25)
    hidden_here = up_weight.shape[1]
    token_rows = tokens.reshape(-1, model_width)
    token_count = token_rows.shape[0]
    core = lax.axis_index("core")

    up_turned = share_pieces(up_weight.T)
    down = share_pieces(down_weight)
    up_bias_here = share_pieces(up_bias[:, None])[:, 0].astype(jnp.float32)

    projection = lax.dynamic_index_in_dim(
        feature_bank, swap_step[0] % feature_bank.shape[0], 0, keepdims=False
    )
    lift_matrix, back_matrix, sums = pair_matrices(projection)
    entries = entry_rows(position_logits)
    seg_col = jnp.broadcast_to(segment_ids[:, :, None], (rows_here, length, LANES))
    seg_row = segment_ids[:, None, :]

    queries = (
        (
            jnp.dot(token_rows, query_weight, preferred_element_type=jnp.float32)
            + query_bias.astype(jnp.float32)
        )
        * query_scale
    ).astype(LOW)
    keys_all = (
        jnp.dot(token_rows, key_weight, preferred_element_type=jnp.float32) * query_scale
    ).astype(LOW)
    values = (
        jnp.dot(token_rows, value_weight, preferred_element_type=jnp.float32)
        + value_bias.astype(jnp.float32)
    ).astype(LOW)
    mixed_out, inverse = attend(
        queries, keys_all, values, seg_col, seg_row, lift_matrix, entries, head_size, REACH,
        rows_here,
    )
    branch = jnp.dot(mixed_out, out_weight, preferred_element_type=jnp.float32) + out_bias.astype(
        jnp.float32
    )
    first_factor = first_gain.astype(jnp.float32)
    hidden, first_normed, first_inverse = normalize(
        token_rows.astype(jnp.float32) + branch, first_factor, first_shift.astype(jnp.float32)
    )
    hidden_low = hidden.astype(LOW)
    hidden_pair = jnp.concatenate([hidden_low, other(hidden_low)], axis=0)
    upward = dot_last(hidden_pair, up_turned) + up_bias_here
    activated = jax.nn.gelu(upward, approximate=False).astype(LOW)
    theirs = jnp.dot(activated[token_count:], down, preferred_element_type=jnp.float32)
    feed_out = jnp.dot(
        activated[:token_count], down, preferred_element_type=jnp.float32
    ) + other(theirs)
    second_factor = second_gain.astype(jnp.float32)
    summed = hidden + feed_out + down_bias.astype(jnp.float32)
    layer_out, second_normed, second_inverse = normalize(
        summed, second_factor, second_shift.astype(jnp.float32)
    )
    upstream = out_cotangent.reshape(-1, model_width).astype(jnp.float32)
    grad_summed, grad_second_gain, grad_second_shift = norm_back(
        upstream, second_normed, second_inverse, second_factor
    )
    grad_down_bias = jnp.sum(grad_summed, axis=0)
    grad_feed = grad_summed.astype(LOW)

    def gelu_exact(inputs):
        return jax.nn.gelu(inputs, approximate=False)

    grad_pair = jnp.concatenate([grad_feed, other(grad_feed)], axis=0)
    part_down_weight = dot_first(activated, grad_pair)
    grad_down_weight = scatter_pieces(part_down_weight)
    grad_act = dot_last(grad_pair, down)
    grad_upward = jax.vjp(gelu_exact, upward)[1](grad_act)[0].astype(LOW)
    part_up_turned = dot_first(grad_upward, hidden_pair)
    grad_up_weight = scatter_pieces(part_up_turned).T
    part_up_bias = jnp.sum(grad_upward.astype(jnp.float32), axis=0)
    back_theirs = jnp.dot(
        grad_upward[token_count:], up_turned, preferred_element_type=jnp.float32
    )
    grad_hidden = (
        grad_summed
        + jnp.dot(grad_upward[:token_count], up_turned, preferred_element_type=jnp.float32)
        + other(back_theirs)
    )
    grad_residual, grad_first_gain, grad_first_shift = norm_back(
        grad_hidden, first_normed, first_inverse, first_factor
    )
    grad_branch = grad_residual.astype(LOW)
    grad_out_bias = jnp.sum(grad_branch.astype(jnp.float32), axis=0)
    grad_out_weight = dot_first(mixed_out, grad_branch)
    grad_mixed = dot_last(grad_branch, out_weight).astype(LOW)
    multiple = 2 * lax.axis_size(GROUP)
    bias_pair = jnp.zeros((2,) + part_up_bias.shape, jnp.float32).at[core].set(part_up_bias)
    early = [
        grad_out_bias,
        grad_first_gain,
        grad_first_shift,
        grad_down_bias,
        grad_second_gain,
        grad_second_shift,
        bias_pair,
    ]
    early_sum = sum_everywhere(
        jnp.concatenate([grad_out_weight, pack_rows(early, model_width, multiple)], axis=0)
    )

    grad_queries, grad_keys, grad_values, turned_logits = attend_back(
        queries, keys_all, values, grad_mixed, mixed_out, inverse, seg_col, seg_row, lift_matrix,
        back_matrix, sums, entries, head_size, REACH, rows_here,
    )
    grad_query_weight = dot_first(token_rows, grad_queries) * query_scale
    grad_query_bias = jnp.sum(grad_queries.astype(jnp.float32), axis=0) * query_scale
    grad_key_weight = dot_first(token_rows, grad_keys) * query_scale
    grad_value_weight = dot_first(token_rows, grad_values)
    grad_value_bias = jnp.sum(grad_values.astype(jnp.float32), axis=0)
    late = [grad_query_bias, grad_value_bias, turned_logits]
    late_sum = sum_everywhere(
        jnp.concatenate(
            [
                grad_query_weight,
                grad_key_weight,
                grad_value_weight,
                pack_rows(late, model_width, multiple),
            ],
            axis=0,
        )
    )
    grad_tokens = (
        grad_residual
        + query_scale * (dot_last(grad_queries, query_weight) + dot_last(grad_keys, key_weight))
        + dot_last(grad_values, value_weight)
    )
    early_out = unpack_rows(early_sum[model_width:], [v.shape for v in early])
    late_out = unpack_rows(late_sum[3 * model_width :], [v.shape for v in late])
    pieces = lax.axis_size("dp")
    bias_all = early_out[6].reshape(2, pieces, lax.axis_size("mq"), hidden_here // pieces)
    grad_up_bias = lax.dynamic_index_in_dim(
        lax.dynamic_index_in_dim(bias_all, core, 0, keepdims=False),
        lax.axis_index("mq"),
        1,
        keepdims=False,
    ).reshape(-1)
    return (
        layer_out.astype(LOW).reshape(rows_here, length, model_width),
        grad_tokens.reshape(rows_here, length, model_width),
        late_sum[:model_width],
        late_out[0],
        late_sum[model_width : 2 * model_width],
        late_sum[2 * model_width : 3 * model_width],
        late_out[1],
        early_sum[:model_width],
        early_out[0],
        entry_grads(late_out[2]),
        early_out[1],
        early_out[2],
        grad_up_weight,
        grad_up_bias,
        grad_down_weight,
        early_out[3],
        early_out[4],
        early_out[5],
    )


REACH = 2


def solution(mesh):
    groups, parts = mesh.devices.shape
    cores = jax.sharding.Mesh(mesh.devices.reshape(groups, parts // 2, 2), ("dp", "mq", "core"))
    rows = ("dp", "mq", "core")
    units = ("mq", "core")
    whole = P()
    in_specs = (
        (P(rows, None, None), P(rows, None))
        + (whole,) * 12
        + (P(None, units), P(units), P(units, None))
        + (whole,) * 3
        + (P(rows, None, None),)
    )
    out_specs = (
        (P(rows, None, None), P(rows, None, None))
        + (whole,) * 10
        + (P(None, units), P(units), P(units, None))
        + (whole,) * 3
    )
    return jax.shard_map(local, mesh=cores, in_specs=in_specs, out_specs=out_specs, check_vma=False)
```

```python
import functools
import jax
import jax.numpy as jnp
from jax import lax
from jax.experimental import pallas as pl
from jax.experimental.pallas import tpu as pltpu
from jax.sharding import PartitionSpec as P

LANES = 128
LOW = jnp.bfloat16


def dot_last(left_side, right_side):
    return lax.dot_general(
        left_side, right_side, (((1,), (1,)), ((), ())), preferred_element_type=jnp.float32
    )


def dot_first(left_side, right_side):
    return lax.dot_general(
        left_side, right_side, (((0,), (0,)), ((), ())), preferred_element_type=jnp.float32
    )


def split_low(wide):
    high = wide.astype(LOW)
    return high, (wide - high.astype(jnp.float32)).astype(LOW)


def key_span(block, blocks, reach):
    first = max(0, block - reach)
    last = min(blocks, block + reach + 1)
    return first * LANES, last * LANES


def features(rows, lift_matrix, gain):
    wide = rows.astype(jnp.float32)
    high, rest = split_low(wide * wide)
    stacked = jnp.concatenate([rows, high, rest], axis=1)
    lifted = jnp.dot(stacked, lift_matrix, preferred_element_type=jnp.float32)
    return jnp.exp(lifted) * gain


def strip(entry_row):
    return pltpu.roll(
        jnp.broadcast_to(entry_row, (LANES, entry_row.shape[1])), 0, 1, stride=1, stride_axis=0
    )


def unstrip(total):
    width = total.shape[1]
    half = total.shape[0] // 2
    while half >= 8:
        total = total[:half] + pltpu.roll(total[half:], width - half, 1)
        half //= 2
    row = lax.broadcasted_iota(jnp.int32, total.shape, 0)
    for step in (4, 2, 1):
        total = jnp.where((row & step) != 0, pltpu.roll(total, width - step, 1), total)
    return jnp.sum(total, axis=0, keepdims=True)


def masked_strip(strip_ref, head, seg_col, seg_row, block, blocks, reach):
    first, last = key_span(block, blocks, reach)
    shift = (blocks - 1 - block) * LANES
    columns = seg_col[block * LANES : (block + 1) * LANES]
    same = jnp.concatenate(
        [
            columns == seg_row[:, start : start + LANES]
            for start in range(first, last, LANES)
        ],
        axis=1,
    )
    return jnp.where(same, strip_ref[head, :, first + shift : last + shift], 0.0)


def attend_kernel(
    head_size, reach, q_ref, k_ref, v_ref, col_ref, row_ref, lift_ref, entry_ref,
    mixed_ref, inverse_ref, strip_ref,
):
    length = q_ref.shape[0]
    blocks = length // LANES
    gain = head_size ** (-0.5)
    for head in range(2):
        strip_ref[head] = strip(entry_ref[0, head : head + 1])
    lift_matrix = lift_ref[0]
    query_low = features(q_ref[...], lift_matrix, gain).astype(LOW)
    key_low = features(k_ref[...], lift_matrix, gain).astype(LOW)
    extended = jnp.concatenate([v_ref[...], jnp.ones((length, LANES), LOW)], axis=1)
    lane = lax.broadcasted_iota(jnp.int32, (LANES, LANES), 1)
    seg_row = row_ref[0]
    seg_col = col_ref[0]
    for block in range(blocks):
        first, last = key_span(block, blocks, reach)
        here = slice(block * LANES, (block + 1) * LANES)
        outs = []
        for head in range(2):
            mine = (lane < head_size) == (head == 0)
            block_query = jnp.where(mine, query_low[here], jnp.zeros((), LOW))
            kernel = dot_last(block_query, key_low[first:last])
            weights = kernel * masked_strip(strip_ref, head, seg_col, seg_row, block, blocks, reach)
            outs.append(
                jnp.dot(
                    weights.astype(LOW), extended[first:last], preferred_element_type=jnp.float32
                )
            )
        both = jnp.where(
            jnp.concatenate([lane, lane], axis=1) % LANES < head_size, outs[0], outs[1]
        )
        inverse = 1.0 / both[:, LANES:]
        mixed_ref[here, :] = (both[:, :LANES] * inverse).astype(LOW)
        inverse_ref[here, :] = inverse


def attend_back_kernel(
    head_size, reach, q_ref, k_ref, v_ref, g_ref, mixed_ref, inverse_ref, col_ref, row_ref,
    lift_ref, back_ref, sums_ref, entry_ref,
    gq_ref, gk_ref, gv_ref, logit_ref, strip_ref, diag_ref, value_acc, key_acc,
):
    length = q_ref.shape[0]
    blocks = length // LANES
    gain = head_size ** (-0.5)
    for head in range(2):
        strip_ref[head] = strip(entry_ref[0, head : head + 1])

    @pl.when(pl.program_id(1) == 0)
    def _():
        diag_ref[...] = jnp.zeros_like(diag_ref)

    lift_matrix = lift_ref[0]
    query_feat = features(q_ref[...], lift_matrix, gain)
    key_feat = features(k_ref[...], lift_matrix, gain)
    query_low = query_feat.astype(LOW)
    key_low = key_feat.astype(LOW)
    values = v_ref[...]
    grad_numer = g_ref[...].astype(jnp.float32) * inverse_ref[...]
    grad_low = grad_numer.astype(LOW)
    high, rest = split_low(grad_numer * mixed_ref[...].astype(jnp.float32))
    grad_denom = jnp.dot(
        jnp.concatenate([high, rest], axis=1), sums_ref[...], preferred_element_type=jnp.float32
    )
    lane = lax.broadcasted_iota(jnp.int32, (LANES, LANES), 1)
    seg_row = row_ref[0]
    seg_col = col_ref[0]
    value_acc[...] = jnp.zeros_like(value_acc)
    key_acc[...] = jnp.zeros_like(key_acc)
    grad_qfeat = []
    for block in range(blocks):
        first, last = key_span(block, blocks, reach)
        shift = (blocks - 1 - block) * LANES
        here = slice(block * LANES, (block + 1) * LANES)
        outs = []
        for head in range(2):
            mine = (lane < head_size) == (head == 0)
            block_query = jnp.where(mine, query_low[here], jnp.zeros((), LOW))
            block_grad = jnp.where(mine, grad_low[here], jnp.zeros((), LOW))
            table = masked_strip(strip_ref, head, seg_col, seg_row, block, blocks, reach)
            weights = dot_last(block_query, key_low[first:last]) * table
            denom = grad_denom[here, head * LANES : (head + 1) * LANES]
            grad_weights = dot_last(block_grad, values[first:last]) - jnp.concatenate(
                [denom] * ((last - first) // LANES), axis=1
            )
            grad_kernel = (grad_weights * table).astype(LOW)
            diag_ref[head, :, first + shift : last + shift] += grad_weights * weights
            value_acc[first:last] += dot_first(weights.astype(LOW), block_grad)
            outs.append(
                jnp.dot(grad_kernel, key_low[first:last], preferred_element_type=jnp.float32)
            )
            key_acc[first:last] += dot_first(grad_kernel, block_query)
        grad_qfeat.append(jnp.where(lane < head_size, outs[0], outs[1]))
    gv_ref[...] = value_acc[...].astype(LOW)

    def lift_back(rows, feature, grad_feature):
        product = grad_feature * feature
        high, rest = split_low(product)
        both = jnp.dot(
            jnp.concatenate([high, rest], axis=1), back_ref[0], preferred_element_type=jnp.float32
        )
        return (both[:, :LANES] - rows.astype(jnp.float32) * both[:, LANES:]).astype(LOW)

    gq_ref[...] = lift_back(q_ref[...], query_feat, jnp.concatenate(grad_qfeat, axis=0))
    gk_ref[...] = lift_back(k_ref[...], key_feat, key_acc[...])
    logit_ref[0] = jnp.concatenate([unstrip(diag_ref[head]) for head in range(2)], axis=0)


def pair_matrices(projection):
    heads, head_size, feat = projection.shape
    pairs = projection.reshape(heads // 2, 2, head_size, feat)
    zero = jnp.zeros_like(pairs[:, 0])
    top = jnp.concatenate([pairs[:, 0], zero], axis=2)
    bottom = jnp.concatenate([zero, pairs[:, 1]], axis=2)
    diagonal = jnp.concatenate([top, bottom], axis=1)
    half = jnp.arange(2 * head_size) // head_size
    ones = jnp.broadcast_to(
        (half[:, None] == half[None, :]).astype(LOW), (heads // 2, 2 * head_size, 2 * feat)
    )
    lift_matrix = jnp.concatenate([diagonal, -0.5 * ones, -0.5 * ones], axis=1).astype(LOW)
    turned = jnp.swapaxes(diagonal, 1, 2)
    back_matrix = jnp.concatenate(
        [
            jnp.concatenate([turned, ones], axis=2),
            jnp.concatenate([jnp.zeros_like(turned), ones], axis=2),
        ],
        axis=1,
    )
    picked = (half[:, None] == (jnp.arange(4 * head_size) // (2 * head_size))[None, :]).astype(LOW)
    sums = jnp.concatenate([picked, picked], axis=0)
    return lift_matrix, back_matrix, sums


def entry_rows(position_logits):
    heads, span = position_logits.shape
    entries = jnp.exp(position_logits.astype(jnp.float32))
    padded = jnp.concatenate([entries, jnp.zeros((heads, 1), jnp.float32)], axis=1)
    turned = jnp.roll(padded[:, ::-1], -LANES, axis=1)
    return turned.reshape(heads // 2, 2, span + 1)


def entry_grads(turned):
    pairs, _, width = turned.shape
    flat = turned.reshape(2 * pairs, width)
    return jnp.roll(flat[:, ::-1], -LANES, axis=1)[:, : width - 1]


def attend(queries, keys, values, seg_col, seg_row, lift_matrix, entries, head_size, reach, rows):
    total, width = queries.shape
    length = total // rows
    pairs = width // LANES
    tile = pl.BlockSpec((length, LANES), lambda p, r: (r, p))
    specs = [
        tile, tile, tile,
        pl.BlockSpec((1, length, LANES), lambda p, r: (r, 0, 0)),
        pl.BlockSpec((1, 1, length), lambda p, r: (r, 0, 0)),
        pl.BlockSpec((1,) + lift_matrix.shape[1:], lambda p, r: (p, 0, 0)),
        pl.BlockSpec((1,) + entries.shape[1:], lambda p, r: (p, 0, 0)),
    ]
    return pl.pallas_call(
        functools.partial(attend_kernel, head_size, reach),
        grid=(pairs, rows),
        in_specs=specs,
        out_specs=[tile, tile],
        out_shape=[
            jax.ShapeDtypeStruct((total, width), LOW),
            jax.ShapeDtypeStruct((total, width), jnp.float32),
        ],
        scratch_shapes=[pltpu.VMEM((2, LANES, entries.shape[2]), jnp.float32)],
        name="attend",
    )(queries, keys, values, seg_col, seg_row, lift_matrix, entries)


def attend_back(
    queries, keys, values, grads, mixed, inverse, seg_col, seg_row, lift_matrix, back_matrix,
    sums, entries, head_size, reach, rows,
):
    total, width = queries.shape
    length = total // rows
    pairs = width // LANES
    tile = pl.BlockSpec((length, LANES), lambda p, r: (r, p))
    specs = [
        tile, tile, tile, tile, tile, tile,
        pl.BlockSpec((1, length, LANES), lambda p, r: (r, 0, 0)),
        pl.BlockSpec((1, 1, length), lambda p, r: (r, 0, 0)),
        pl.BlockSpec((1,) + lift_matrix.shape[1:], lambda p, r: (p, 0, 0)),
        pl.BlockSpec((1,) + back_matrix.shape[1:], lambda p, r: (p, 0, 0)),
        pl.BlockSpec(sums.shape, lambda p, r: (0, 0)),
        pl.BlockSpec((1,) + entries.shape[1:], lambda p, r: (p, 0, 0)),
    ]
    low_out = jax.ShapeDtypeStruct((total, width), LOW)
    span = entries.shape[2]
    return pl.pallas_call(
        functools.partial(attend_back_kernel, head_size, reach),
        grid=(pairs, rows),
        in_specs=specs,
        out_specs=[tile, tile, tile, pl.BlockSpec((1, 2, span), lambda p, r: (p, 0, 0))],
        out_shape=[low_out, low_out, low_out, jax.ShapeDtypeStruct((pairs, 2, span), jnp.float32)],
        scratch_shapes=[
            pltpu.VMEM((2, LANES, span), jnp.float32),
            pltpu.VMEM((2, LANES, span), jnp.float32),
            pltpu.VMEM((length, LANES), jnp.float32),
            pltpu.VMEM((length, LANES), jnp.float32),
        ],
        name="attend_back",
    )(
        queries, keys, values, grads, mixed, inverse, seg_col, seg_row, lift_matrix, back_matrix,
        sums, entries,
    )


EPSILON = 1e-05


def normalize(inputs, factor, offset):
    centre = inputs - jnp.mean(inputs, axis=-1, keepdims=True)
    spread = jnp.mean(centre * centre, axis=-1, keepdims=True)
    inverse = lax.rsqrt(spread + EPSILON)
    normed = centre * inverse
    return (normed * factor + offset, normed, inverse)


def norm_back(upstream, normed, inverse, factor):
    scaled = upstream * factor
    inner = (
        scaled
        - jnp.mean(scaled, axis=-1, keepdims=True)
        - normed * jnp.mean(scaled * normed, axis=-1, keepdims=True)
    )
    return (inverse * inner, jnp.sum(upstream * normed, axis=0), jnp.sum(upstream, axis=0))


def send(array, axis, step):
    size = lax.axis_size(axis)
    return lax.ppermute(array, axis, [(i, (i + step) % size) for i in range(size)])


def other(array):
    return send(array, "core", 1)


def gather_axis(array, axis):
    return jnp.concatenate(
        [array] + [send(array, axis, step) for step in range(1, lax.axis_size(axis))], axis=0
    )


def scatter_axis(array, axis):
    size = lax.axis_size(axis)
    blocks = jnp.split(array, size, axis=0)
    total = blocks[0].astype(jnp.float32)
    for step in range(1, size):
        total = total + send(blocks[step], axis, size - step).astype(jnp.float32)
    return total.astype(array.dtype)


def in_order(blocks, axis):
    size = lax.axis_size(axis)
    here = lax.axis_index(axis)
    if size == 2:
        return jnp.concatenate(
            [jnp.where(here == 0, blocks[0], blocks[1]), jnp.where(here == 0, blocks[1], blocks[0])],
            axis=0,
        )
    turned = jnp.concatenate(blocks[::-1] + blocks[::-1], axis=0)
    rows = blocks[0].shape[0]
    return lax.dynamic_slice_in_dim(turned, (size - 1 - here) * rows, size * rows, 0)


def gather_in_order(array, axis):
    steps = range(1, lax.axis_size(axis))
    return in_order([array] + [send(array, axis, step) for step in steps], axis)


def scatter_in_order(array, axis):
    size = lax.axis_size(axis)
    here = lax.axis_index(axis)
    rows = array.shape[0] // size
    total = lax.dynamic_slice_in_dim(array, here * rows, rows, 0).astype(jnp.float32)
    for step in range(1, size):
        block = lax.dynamic_slice_in_dim(array, ((here + step) % size) * rows, rows, 0)
        total = total + send(block, axis, step).astype(jnp.float32)
    return total.astype(array.dtype)


ROUTES = (("y", "dp"), ("dp", "y"))


def own_piece(array):
    piece = array.shape[0] // lax.axis_size("dp")
    return lax.dynamic_slice_in_dim(array, lax.axis_index("dp") * piece, piece, 0)


def share_pieces(array):
    piece = own_piece(array)
    half = piece.shape[0] // 2
    steps = range(1, lax.axis_size("z"))
    levels = [piece] + [send(piece, "z", step) for step in steps]
    parts = []
    for part, route in enumerate(ROUTES):
        rows = jnp.concatenate([x[part * half : (part + 1) * half] for x in levels], axis=0)
        for axis in route:
            rows = gather_axis(rows, axis)
        parts.append(rows)
    return jnp.concatenate(parts, axis=0)


def scatter_pieces(array):
    halves = []
    for rows, route in zip(jnp.split(array.astype(LOW), 2, axis=0), ROUTES):
        for axis in route[::-1]:
            rows = scatter_axis(rows, axis)
        halves.append(rows)
    size = lax.axis_size("z")
    half = halves[0].shape[0] // size
    levels = [
        jnp.concatenate([x[k * half : (k + 1) * half] for x in halves], axis=0)
        for k in range(size)
    ]
    total = levels[0].astype(jnp.float32)
    for step in range(1, size):
        total = total + send(levels[step], "z", size - step).astype(jnp.float32)
    return gather_in_order(total.astype(LOW), "dp").astype(jnp.float32)


def bias_order(rows):
    shape = (lax.axis_size("dp"), lax.axis_size("y"), lax.axis_size("z"), 2, -1)
    blocks = rows.reshape(shape)
    first = blocks[:, :, :, 0].reshape(-1)
    second = jnp.swapaxes(blocks[:, :, :, 1], 0, 1).reshape(-1)
    return jnp.concatenate([first, second])


def bias_blocks(flat):
    first, second = jnp.split(flat, 2)
    groups, parts, levels = (lax.axis_size(axis) for axis in ("dp", "y", "z"))
    first = first.reshape(groups, parts, levels, -1)
    second = jnp.swapaxes(second.reshape(parts, groups, levels, -1), 0, 1)
    return jnp.stack([first, second], axis=3).reshape(groups * parts * levels, -1)


def share_bias(bias):
    rows = own_piece(bias).astype(jnp.float32)[None]
    for axis in ("z", "y", "dp"):
        rows = gather_axis(rows, axis)
    return bias_order(rows)


def scatter_bias(flat):
    rows = bias_blocks(flat)
    for axis in ("dp", "y", "z"):
        rows = scatter_axis(rows, axis)
    return gather_in_order(rows, "dp").reshape(-1)


def sum_everywhere(array):
    half = array.shape[0] // 2
    core = lax.axis_index("core")
    low = array.astype(LOW)
    keep = lax.dynamic_slice_in_dim(low, core * half, half, 0)
    give = lax.dynamic_slice_in_dim(low, (1 - core) * half, half, 0)
    pair = (keep.astype(jnp.float32) + other(give).astype(jnp.float32)).astype(LOW)
    parts = []
    for columns, route in zip(jnp.split(pair, 2, axis=1), ROUTES):
        order = route[::-1] + ("z",)
        for axis in order:
            columns = scatter_in_order(columns, axis)
        for axis in order[::-1]:
            columns = gather_in_order(columns, axis)
        parts.append(columns)
    return gather_in_order(jnp.concatenate(parts, axis=1), "core").astype(jnp.float32)


def sum_small(array):
    for axis in ("core", "dp", "y", "z"):
        size = lax.axis_size(axis)
        step = 1
        while step < size:
            array = array + lax.ppermute(array, axis, [(i, i ^ step) for i in range(size)])
            step *= 2
    return array


def pack_rows(vectors):
    flat = jnp.concatenate([v.reshape(-1) for v in vectors])
    rows = -(-flat.shape[0] // (8 * LANES)) * 8
    return jnp.pad(flat, (0, rows * LANES - flat.shape[0])).reshape(rows, LANES)


def unpack_rows(packed, shapes):
    flat = packed.reshape(-1)
    out, at = [], 0
    for shape in shapes:
        size = 1
        for extent in shape:
            size *= extent
        out.append(flat[at : at + size].reshape(shape))
        at += size
    return out


def local(
    tokens,
    segment_ids,
    swap_step,
    feature_bank,
    query_weight,
    query_bias,
    key_weight,
    value_weight,
    value_bias,
    out_weight,
    out_bias,
    position_logits,
    first_gain,
    first_shift,
    up_weight,
    up_bias,
    down_weight,
    down_bias,
    second_gain,
    second_shift,
    out_cotangent,
):
    rows_here, length, model_width = tokens.shape
    head_count = position_logits.shape[0]
    head_size = model_width // head_count
    query_scale = head_size ** (-0.25)
    token_rows = tokens.reshape(-1, model_width)
    token_count = token_rows.shape[0]

    up_turned = share_pieces(up_weight.T)
    down = share_pieces(down_weight)
    up_bias_here = share_bias(up_bias)

    projection = lax.dynamic_index_in_dim(
        feature_bank, swap_step[0] % feature_bank.shape[0], 0, keepdims=False
    )
    lift_matrix, back_matrix, sums = pair_matrices(projection)
    entries = entry_rows(position_logits)
    seg_col = jnp.broadcast_to(segment_ids[:, :, None], (rows_here, length, LANES))
    seg_row = segment_ids[:, None, :]

    queries = (
        (
            jnp.dot(token_rows, query_weight, preferred_element_type=jnp.float32)
            + query_bias.astype(jnp.float32)
        )
        * query_scale
    ).astype(LOW)
    keys_all = (
        jnp.dot(token_rows, key_weight, preferred_element_type=jnp.float32) * query_scale
    ).astype(LOW)
    values = (
        jnp.dot(token_rows, value_weight, preferred_element_type=jnp.float32)
        + value_bias.astype(jnp.float32)
    ).astype(LOW)
    mixed_out, inverse = attend(
        queries, keys_all, values, seg_col, seg_row, lift_matrix, entries, head_size, REACH,
        rows_here,
    )
    branch = jnp.dot(mixed_out, out_weight, preferred_element_type=jnp.float32) + out_bias.astype(
        jnp.float32
    )
    first_factor = first_gain.astype(jnp.float32)
    hidden, first_normed, first_inverse = normalize(
        token_rows.astype(jnp.float32) + branch, first_factor, first_shift.astype(jnp.float32)
    )
    hidden_low = hidden.astype(LOW)
    hidden_pair = jnp.concatenate([hidden_low, other(hidden_low)], axis=0)
    upward = dot_last(hidden_pair, up_turned) + up_bias_here
    activated = jax.nn.gelu(upward, approximate=False).astype(LOW)
    theirs = jnp.dot(activated[token_count:], down, preferred_element_type=jnp.float32)
    feed_out = jnp.dot(
        activated[:token_count], down, preferred_element_type=jnp.float32
    ) + other(theirs)
    second_factor = second_gain.astype(jnp.float32)
    summed = hidden + feed_out + down_bias.astype(jnp.float32)
    layer_out, second_normed, second_inverse = normalize(
        summed, second_factor, second_shift.astype(jnp.float32)
    )
    upstream = out_cotangent.reshape(-1, model_width).astype(jnp.float32)
    grad_summed, grad_second_gain, grad_second_shift = norm_back(
        upstream, second_normed, second_inverse, second_factor
    )
    grad_down_bias = jnp.sum(grad_summed, axis=0)
    grad_feed = grad_summed.astype(LOW)

    def gelu_exact(inputs):
        return jax.nn.gelu(inputs, approximate=False)

    grad_pair = jnp.concatenate([grad_feed, other(grad_feed)], axis=0)
    part_down_weight = dot_first(activated, grad_pair)
    grad_down_weight = scatter_pieces(part_down_weight)
    grad_act = dot_last(grad_pair, down)
    grad_upward = jax.vjp(gelu_exact, upward)[1](grad_act)[0].astype(LOW)
    part_up_turned = dot_first(grad_upward, hidden_pair)
    grad_up_weight = scatter_pieces(part_up_turned).T
    grad_up_bias = scatter_bias(jnp.sum(grad_upward.astype(jnp.float32), axis=0))
    back_theirs = jnp.dot(
        grad_upward[token_count:], up_turned, preferred_element_type=jnp.float32
    )
    grad_hidden = (
        grad_summed
        + jnp.dot(grad_upward[:token_count], up_turned, preferred_element_type=jnp.float32)
        + other(back_theirs)
    )
    grad_residual, grad_first_gain, grad_first_shift = norm_back(
        grad_hidden, first_normed, first_inverse, first_factor
    )
    grad_branch = grad_residual.astype(LOW)
    grad_out_bias = jnp.sum(grad_branch.astype(jnp.float32), axis=0)
    grad_out_weight = dot_first(mixed_out, grad_branch)
    grad_mixed = dot_last(grad_branch, out_weight).astype(LOW)
    early = [
        grad_out_bias,
        grad_first_gain,
        grad_first_shift,
        grad_down_bias,
        grad_second_gain,
        grad_second_shift,
    ]
    early_out = unpack_rows(sum_small(pack_rows(early)), [v.shape for v in early])
    grad_out_weight = sum_everywhere(grad_out_weight)

    grad_queries, grad_keys, grad_values, turned_logits = attend_back(
        queries, keys_all, values, grad_mixed, mixed_out, inverse, seg_col, seg_row, lift_matrix,
        back_matrix, sums, entries, head_size, REACH, rows_here,
    )
    grad_query_weight = dot_first(token_rows, grad_queries) * query_scale
    grad_query_bias = jnp.sum(grad_queries.astype(jnp.float32), axis=0) * query_scale
    grad_key_weight = dot_first(token_rows, grad_keys) * query_scale
    grad_value_weight = dot_first(token_rows, grad_values)
    grad_value_bias = jnp.sum(grad_values.astype(jnp.float32), axis=0)
    late = [grad_query_bias, grad_value_bias, turned_logits]
    late_out = unpack_rows(sum_small(pack_rows(late)), [v.shape for v in late])
    late_sum = sum_everywhere(
        jnp.concatenate(
            [
                grad_query_weight.astype(LOW),
                grad_key_weight.astype(LOW),
                grad_value_weight.astype(LOW),
            ],
            axis=0,
        )
    )
    grad_tokens = (
        grad_residual
        + query_scale * (dot_last(grad_queries, query_weight) + dot_last(grad_keys, key_weight))
        + dot_last(grad_values, value_weight)
    )
    return (
        layer_out.astype(LOW).reshape(rows_here, length, model_width),
        grad_tokens.reshape(rows_here, length, model_width),
        late_sum[:model_width],
        late_out[0],
        late_sum[model_width : 2 * model_width],
        late_sum[2 * model_width : 3 * model_width],
        late_out[1],
        grad_out_weight,
        early_out[0],
        entry_grads(late_out[2]),
        early_out[1],
        early_out[2],
        grad_up_weight,
        grad_up_bias,
        grad_down_weight,
        early_out[3],
        early_out[4],
        early_out[5],
    )


REACH = 2


def solution(mesh):
    groups, parts = mesh.devices.shape
    levels = min(4, parts // 2)
    cores = jax.sharding.Mesh(
        mesh.devices.reshape(groups, levels, parts // (2 * levels), 2), ("dp", "z", "y", "core")
    )
    rows = ("dp", "z", "y", "core")
    units = ("z", "y", "core")
    whole = P()
    in_specs = (
        (P(rows, None, None), P(rows, None))
        + (whole,) * 12
        + (P(None, units), P(units), P(units, None))
        + (whole,) * 3
        + (P(rows, None, None),)
    )
    out_specs = (
        (P(rows, None, None), P(rows, None, None))
        + (whole,) * 10
        + (P(None, units), P(units), P(units, None))
        + (whole,) * 3
    )
    return jax.shard_map(local, mesh=cores, in_specs=in_specs, out_specs=out_specs, check_vma=False)
```
